512 devices in a mesh: rep: 16 (over x, y_lo), shard: 32 (over z, y_hi, core).
Axes of the slice: x: 4, y: 8 (y_hi: 2, y_lo: 4; y = y_hi * 4 + y_lo), z: 8, core: 2. Of those that a mesh axis runs over, the one named last changes fastest.
Arguments:
- inner_weights: float32 [16, 2, 512, 512], P('rep', None, 'shard'), may hold values from -6 to 6
- first_moment: float32 [16, 2, 512, 512], P('rep', None, 'shard'), may hold values from -1 to 1
- second_moment: float32 [16, 2, 512, 512], P('rep', None, 'shard'), may hold values from 0 to 1, as said below
- outer_weights: float32 [2, 512, 512], P(None, 'shard'), may hold values from -6 to 6
- outer_velocity: float32 [2, 512, 512], P(None, 'shard'), may hold values from -3 to 3
- tokens: bfloat16 [16, 2, 16384, 512], P('rep', None, 'shard'), may hold values from -6 to 6
- targets: bfloat16 [16, 2, 16384, 2, 512], P('rep', None, 'shard'), may hold values from -25 to 25
- step_count: int32 [1], replicated, may hold values from 10 to 39
- first_fragment: int32 [1], replicated, may hold values from 0 to 1
Outputs:
- new_outer: float32 [2, 512, 512], P(None, 'shard')
- new_inner: float32 [16, 2, 512, 512], P('rep', None, 'shard')
The draws below stay inside these ranges and needn't reach their ends.
Inputs may be any that keep to these rules, and one draw needn't show every extreme that they name: `second_moment`: positive.
All inputs are finite; a program needn't handle non-finite values.
Results may differ from the reference program's by a relative error of at most 0.00085.
Values may be sent and summed in bfloat16 or wider, within the bound.
A program may use at most 64 MiB of HBM per device.

```python
import math
import jax
import jax.numpy as jnp
from jax import lax

D = 512
STEPS = 2
FRAG = 512
TOKENS = 16384
N_REP = 16
N_SHARD = 32


def clipped_scale():
    return 0.02 / math.sqrt(2.0 * FRAG * D)


def draw_first_moment(key, part):
    dims = (N_REP, 2, FRAG, D)
    spread = 0.15 * clipped_scale()
    return spread * jax.random.truncated_normal(key, -4.0, 4.0, dims, jnp.float32)


def draw_second_moment(key, part):
    dims = (N_REP, 2, FRAG, D)
    square = clipped_scale() * clipped_scale()
    lowest = math.log(0.01)
    highest = math.log(0.1)
    return square * jnp.exp(jax.random.uniform(key, dims, jnp.float32, lowest, highest))


def draw_targets(key, part):
    dims = (N_REP, STEPS, TOKENS, 2, FRAG)
    position = jnp.arange(FRAG, dtype=jnp.float32) / max(FRAG - 1, 1)
    growth = 0.5 * jnp.exp(math.log(8.0) * position)
    return (growth * jax.random.truncated_normal(key, -4.0, 4.0, dims, jnp.float32)).astype(jnp.bfloat16)


def levels(key, shape, shards, smallest, top_value):
    factor_of, own = 1.0, jax.random.fold_in(key, 6)
    for axis_at, blocks in shards:
        steps = jnp.exp(jax.random.uniform(jax.random.fold_in(own, axis_at), (blocks,), jnp.float32, smallest / len(shards), top_value / len(shards)))
        factor_of = factor_of * jnp.repeat(steps, shape[axis_at] // blocks).reshape([-1 if axis == axis_at else 1 for axis in range(len(shape))])
    return factor_of


def normal_values(stream_key, shape, scale, reach, split=(), held_as=jnp.bfloat16):
    factor_of = levels(stream_key, shape, split, -0.22, 0.18) if split else 1.0
    values = jax.random.normal(stream_key, shape, jnp.float32) * scale * factor_of
    return jnp.minimum(jnp.maximum(values, -reach), reach).astype(held_as)


def setup_inputs(seed: int = 0) -> dict:
    keys = jax.random.split(jax.random.key(seed), 10)
    return {
        "inner_weights": normal_values(keys[0], (N_REP, 2, FRAG, D), 1.0, 6.0, ((0, 16), (2, 32)), jnp.float32),
        "first_moment": draw_first_moment(jax.random.fold_in(keys[9], 71), 0),
        "second_moment": draw_second_moment(jax.random.fold_in(keys[9], 71), 0),
        "outer_weights": normal_values(keys[3], (2, FRAG, D), 1.0, 6.0, ((1, 32),), jnp.float32),
        "outer_velocity": normal_values(keys[4], (2, FRAG, D), 0.5, 3.0, ((1, 32),), jnp.float32),
        "tokens": normal_values(keys[5], (N_REP, STEPS, TOKENS, D), 1.0, 6.0, ((0, 16), (2, 32))),
        "targets": draw_targets(jax.random.fold_in(keys[9], 71), 0),
        "step_count": jax.random.randint(keys[7], (1,), 10, 40).astype(jnp.int32),
        "first_fragment": jax.random.randint(keys[8], (1,), 0, 2).astype(jnp.int32),
    }


beta_one = 0.9
beta_two = 0.95
inner_rate = 0.1
adam_eps = 1e-08
decay_rate = 0.1
clip_norm = 0.02
outer_rate = 0.7
outer_momentum = 0.9
mixing = 0.5

def replica_step(weights, moment_one, moment_two, batch, target, count):
    rows = weights.shape[0] * weights.shape[1]
    width = weights.shape[2]
    flat = weights.astype(jnp.bfloat16).reshape(rows, width)
    scale = 1.0 / math.sqrt(width)
    grad_scale = scale / batch.shape[0]
    tok_dev = batch.shape[0] // N_SHARD

    def block(index, total):
        start = (index * tok_dev).astype(jnp.int32)
        piece = lax.dynamic_slice_in_dim(batch, start, tok_dev, 0)
        goal = lax.dynamic_slice_in_dim(target, start, tok_dev, 0).reshape(tok_dev, rows)
        raw = jnp.dot(piece, flat.T, preferred_element_type=jnp.float32) * scale
        residual = (raw - goal.astype(jnp.float32)).astype(jnp.bfloat16)
        term = (jnp.dot(residual.T, piece, preferred_element_type=jnp.float32) * grad_scale).astype(jnp.bfloat16)
        term = lax.optimization_barrier(term)
        return total + term.astype(jnp.float32)
    grad = lax.fori_loop(0, N_SHARD, block, jnp.zeros((rows, width), jnp.float32)).reshape(weights.shape)
    norm = jnp.sqrt(jnp.sum(grad * grad))
    clipped = grad * jnp.minimum(1.0, clip_norm / (norm + 1e-06))
    moment_one = beta_one * moment_one + (1.0 - beta_one) * clipped
    moment_two = beta_two * moment_two + (1.0 - beta_two) * clipped * clipped
    correct_one = 1.0 - jnp.power(beta_one, count)
    correct_two = 1.0 - jnp.power(beta_two, count)
    update = moment_one / correct_one / (jnp.sqrt(moment_two / correct_two) + adam_eps)
    weights = weights - inner_rate * (update + decay_rate * weights)
    return (weights, moment_one, moment_two)

def reference(inner_weights, first_moment, second_moment, outer_weights, outer_velocity, tokens, targets, step_count, first_fragment):
    first = first_fragment[0]
    inner, moment_one, moment_two = (inner_weights, first_moment, second_moment)
    outer, velocity = (outer_weights, outer_velocity)
    for step in range(STEPS):
        frag = first if step == 0 else 1 - first
        theta = lax.dynamic_index_in_dim(outer, frag, 0, keepdims=False)
        speed = lax.dynamic_index_in_dim(velocity, frag, 0, keepdims=False)
        own = lax.dynamic_index_in_dim(inner, frag, 1, keepdims=False)
        delta = lax.optimization_barrier(jnp.sum(theta[None] - own, 0)) / N_REP
        speed = outer_momentum * speed + delta
        theta = theta - outer_rate * (outer_momentum * speed + delta)
        outer = lax.dynamic_update_index_in_dim(outer, theta, frag, 0)
        velocity = lax.dynamic_update_index_in_dim(velocity, speed, frag, 0)
        count = step_count[0].astype(jnp.float32) + step

        def one_replica(items):
            return replica_step(items[0], items[1], items[2], items[3], items[4], count)
        inner, moment_one, moment_two = lax.map(one_replica, (inner, moment_one, moment_two, tokens[:, step], targets[:, step]))
        local = lax.dynamic_index_in_dim(inner, frag, 1, keepdims=False)
        merged = mixing * theta[None] + (1.0 - mixing) * local
        inner = lax.dynamic_update_index_in_dim(inner, merged, frag, 1)
    return (outer, inner)
```

```python
import functools
import math

import jax
import jax.numpy as jnp
from jax import lax
from jax.experimental import pallas as pl
from jax.experimental.pallas import tpu as pltpu
from jax.sharding import PartitionSpec as P

beta_one = 0.9
beta_two = 0.95
inner_rate = 0.1
adam_eps = 1e-08
decay_rate = 0.1
clip_norm = 0.02
outer_rate = 0.7
outer_momentum = 0.9
mixing = 0.5

NZ, NY, NK = 8, 2, 2
NS = NZ * NY * NK
ROWS = 96
HALF = ROWS // 2
F32, BF16 = jnp.float32, jnp.bfloat16


def kernel(
    n_rep,
    scale,
    grad_scale,
    count_ref,
    first_ref,
    part_ref,
    w_ref,
    m_ref,
    v_ref,
    outer_ref,
    vel_ref,
    new_outer_ref,
    new_inner_ref,
    core_in,
    ring_out,
    ring_in,
    total,
    y_out,
    y_in,
    c_tmp,
    c_out,
    c_in,
    c_full,
    gram,
    n_out,
    n_in,
    rep_out,
    rep_in,
    rep_all,
    core_s,
    core_r,
    ring_s,
    ring_r,
    y_s,
    y_r,
    c_s,
    c_r,
    ag_s,
    ag_r,
    fw_s,
    fw_r,
    n_s,
    n_r,
    rs_s,
    rs_r,
    ra_s,
    ra_r,
):
    rep = lax.axis_index("rep")
    me = lax.axis_index("shard")
    z = me // 4
    y = (me // 2) % 2
    k = me % 2

    def at(zz, yy, kk):
        return (rep, zz * 4 + yy * 2 + kk)

    partner = at(z, y, 1 - k)

    def remote(src, dst, ss, rs, dev):
        return pltpu.make_async_remote_copy(
            src_ref=src,
            dst_ref=dst,
            send_sem=ss,
            recv_sem=rs,
            device_id=dev,
            device_id_type=pl.DeviceIdType.MESH,
        )

    barrier = pltpu.get_barrier_semaphore()

    @pl.loop(1, NS)
    def _(o):
        pl.semaphore_signal(
            barrier, inc=1, device_id=(rep, (me + o) % NS), device_id_type=pl.DeviceIdType.MESH
        )

    @pl.loop(1, n_rep)
    def _(o):
        pl.semaphore_signal(
            barrier, inc=1, device_id=((rep + o) % n_rep, me), device_id_type=pl.DeviceIdType.MESH
        )

    pl.semaphore_wait(barrier, NS - 1 + n_rep - 1)

    def rep_send_copy(s, o):
        to = (rep + o) % n_rep
        return remote(rep_out.at[s, to], rep_in.at[s, o], rs_s.at[s, o], rs_r.at[s, o], (to, me))

    def rep_back_copy(s, o, row):
        to = (rep + o) % n_rep
        return remote(rep_all.at[s, row], rep_all.at[s, row], ra_s.at[s, o], ra_r.at[s, o], (to, me))

    def rep_start(s, value):
        rep_out[s] = value.reshape(n_rep, 1, value.shape[-1])

        @pl.loop(1, n_rep)
        def _(o):
            rep_send_copy(s, o).start()

    def rep_middle(s):
        @pl.loop(1, n_rep)
        def _(o):
            rep_send_copy(s, o).wait_recv()

        acc = rep_out[s, rep]
        for o in range(1, n_rep):
            acc = acc + rep_in[s, o]
        rep_all[s, rep] = acc

        @pl.loop(1, n_rep)
        def _(o):
            rep_back_copy(s, o, rep).start()

    def rep_end(s):
        @pl.loop(1, n_rep)
        def _(o):
            rep_back_copy(s, o, (rep + n_rep - o) % n_rep).wait_recv()

        return rep_all[s].reshape(n_rep, rep_all.shape[-1])

    def core_copy(s):
        return remote(part_ref.at[s, 1 - k], core_in.at[s], core_s.at[s], core_r.at[s], partner)

    def ring_copy(s, d, i):
        zz = (z + 1) % NZ if d == 0 else (z + NZ - 1) % NZ
        return remote(
            ring_out.at[s, d, i], ring_in.at[s, d, i], ring_s.at[s, d, i], ring_r.at[s, d, i], at(zz, y, k)
        )

    def own(s, owner, h):
        rows = pl.ds(HALF * h, HALF)
        return part_ref[s, k, owner, rows, :].astype(F32) + core_in[s, owner, rows, :].astype(F32)

    def ring_send(s, d, long, t):
        hops = 4 if long else 3
        i = t if long else 4 + t
        h = d if long else 1 - d
        owner = (z + hops - t) % NZ if d == 0 else (z + NZ - hops + t) % NZ
        val = own(s, owner, h)
        if t > 0:
            ring_copy(s, d, i - 1).wait_recv()
            val = val + ring_in[s, d, i - 1].astype(F32)
        ring_out[s, d, i] = val.astype(BF16)
        ring_copy(s, d, i).start()

    def ring_step(s, t):
        for long in (True, False):
            if long or t < 3:
                for d in range(2):
                    ring_send(s, d, long, t)

    def y_copy(s):
        return remote(y_out.at[s], y_in.at[s], y_s.at[s], y_r.at[s], at(z, 1 - y, k))

    def y_start(s):
        for h in range(2):
            for i, d in ((3, h), (6, 1 - h)):
                ring_copy(s, d, i).wait_recv()
            total[s, pl.ds(HALF * h, HALF), :] = (
                own(s, z, h) + ring_in[s, h, 3].astype(F32) + ring_in[s, 1 - h, 6].astype(F32)
            )
        y_out[s, pl.ds(0, 32), :] = total[s, pl.ds(32 * (1 - y), 32), :].astype(BF16)
        y_out[s, pl.ds(32, 32), :] = total[s, pl.ds(64, 32), :].astype(BF16)
        y_copy(s).start()

    def c_copy(s):
        return remote(c_out.at[s], c_in.at[s], c_s.at[s], c_r.at[s], partner)

    def ag_copy(s, o, src):
        return remote(
            gram.at[s, src, k], gram.at[s, src, k], ag_s.at[s, o], ag_r.at[s, o], at((z + o) % NZ, y, k)
        )

    def fw_copy(s, o, kk):
        src = (z + NZ - o) % NZ
        return remote(gram.at[s, src, kk], gram.at[s, src, kk], fw_s.at[s, o], fw_r.at[s, o], partner)

    def gather_start(s):
        y_copy(s).wait_recv()
        g = total[s, pl.ds(64, 32), :] + y_in[s, pl.ds(32, 32), :].astype(F32)
        gram[s, z, k] = g.astype(BF16)
        for o in (4, 3, 5, 2, 6, 1, 7):
            ag_copy(s, o, z).start()
        fw_copy(s, 0, k).start()
        c_tmp[s] = total[s, pl.ds(32 * y, 32), :] + y_in[s, pl.ds(0, 32), :].astype(F32)
        c_out[s] = c_tmp[s, pl.ds(16 * (1 - k), 16), :].astype(BF16)
        c_copy(s).start()

    def gather_forward(s):
        for o in (1, 7, 2, 6, 3, 5, 4):
            ag_copy(s, o, (z + NZ - o) % NZ).wait_recv()
            fw_copy(s, o, k).start()

    def gather_end(s):
        c_copy(s).wait_recv()
        c_full[s, k] = c_tmp[s, pl.ds(16 * k, 16), :]
        c_full[s, 1 - k] = c_in[s].astype(F32)
        for o in range(NZ):
            fw_copy(s, o, 1 - k).wait_recv()

    def n_copy(s, o):
        return remote(n_out.at[s], n_in.at[s, o], n_s.at[s, o], n_r.at[s, o], (rep, (me + o) % NS))

    def grad_start(s, w):
        flat = w.reshape(32, 512).astype(BF16)
        prod = jnp.dot(flat, gram[s].reshape(512, 512), preferred_element_type=F32)
        g = (prod * scale - c_full[s].reshape(32, 512)) * grad_scale
        n_out[s] = jnp.broadcast_to(jnp.sum(jnp.sum(g * g, axis=0, keepdims=True), axis=1, keepdims=True), (1, 128))

        @pl.loop(1, NS)
        def _(o):
            n_copy(s, o).start()

        return g.reshape(2, 16, 512)

    def clip_factor(s):
        @pl.loop(1, NS)
        def _(o):
            n_copy(s, o).wait_recv()

        acc = n_out[s]
        for o in range(1, NS):
            acc = acc + n_in[s, o]
        f = jnp.minimum(1.0, clip_norm / (jnp.sqrt(acc) + 1e-06))
        return f[:, :1].reshape(1, 1, 1)

    def adam(s, w, m, v, clipped):
        count = jnp.full((1, 8, 128), count_ref[0].astype(F32) + s, F32)
        one = (1.0 - jnp.exp(count * math.log(beta_one)))[:, :1, :1]
        two = (1.0 - jnp.exp(count * math.log(beta_two)))[:, :1, :1]
        m = beta_one * m + (1.0 - beta_one) * clipped
        v = beta_two * v + (1.0 - beta_two) * clipped * clipped
        update = m / one / (jnp.sqrt(v / two) + adam_eps)
        return w - inner_rate * (update + decay_rate * w), m, v

    lead = first_ref[0] == 0

    def outer_step(theta, speed, weight_sum):
        delta = theta - weight_sum * (1.0 / n_rep)
        speed = outer_momentum * speed + delta
        return theta - outer_rate * (outer_momentum * speed + delta)

    w, m, v = w_ref[...], m_ref[...], v_ref[...]
    core_copy(0).start()
    rep_start(0, jnp.where(lead, w[0], w[1]))
    core_copy(1).start()
    core_copy(0).wait_recv()
    for t in range(4):
        ring_step(0, t)
    rep_middle(0)
    y_start(0)
    core_copy(1).wait_recv()
    ring_step(1, 0)
    ring_step(1, 1)
    gather_start(0)
    ring_step(1, 2)
    gather_forward(0)
    ring_step(1, 3)
    gather_end(0)
    g = grad_start(0, w)
    y_start(1)
    clipped = g * clip_factor(0)
    w, m, v = adam(0, w, m, v, clipped)
    rep_start(1, jnp.where(lead, w[1], w[0]))
    theta0 = outer_step(
        jnp.where(lead, outer_ref[0], outer_ref[1]), jnp.where(lead, vel_ref[0], vel_ref[1]), rep_end(0)
    )
    a = jnp.where(lead, mixing * theta0 + (1.0 - mixing) * w[0], w[0])
    b = jnp.where(lead, w[1], mixing * theta0 + (1.0 - mixing) * w[1])
    w = jnp.stack([a, b])
    gather_start(1)
    gather_forward(1)
    gather_end(1)
    g = grad_start(1, w)
    rep_middle(1)
    clipped = g * clip_factor(1)
    w, m, v = adam(1, w, m, v, clipped)
    theta1 = outer_step(
        jnp.where(lead, outer_ref[1], outer_ref[0]), jnp.where(lead, vel_ref[1], vel_ref[0]), rep_end(1)
    )
    new_inner_ref[0] = jnp.where(lead, w[0], mixing * theta1 + (1.0 - mixing) * w[0])
    new_inner_ref[1] = jnp.where(lead, mixing * theta1 + (1.0 - mixing) * w[1], w[1])
    new_outer_ref[0] = jnp.where(lead, theta0, theta1)
    new_outer_ref[1] = jnp.where(lead, theta1, theta0)

    for s in range(2):
        core_copy(s).wait_send()
        y_copy(s).wait_send()
        c_copy(s).wait_send()
        for d in range(2):
            for i in range(7):
                ring_copy(s, d, i).wait_send()
        for o in range(1, NZ):
            ag_copy(s, o, z).wait_send()
        for o in range(NZ):
            fw_copy(s, o, k).wait_send()

        @pl.loop(1, NS)
        def _(o):
            n_copy(s, o).wait_send()

        @pl.loop(1, n_rep)
        def _(o):
            rep_send_copy(s, o).wait_send()
            rep_back_copy(s, o, rep).wait_send()


def body(
    inner_weights,
    first_moment,
    second_moment,
    outer_weights,
    outer_velocity,
    tokens,
    targets,
    step_count,
    first_fragment,
):
    n_rep = lax.axis_size("rep")
    tok_dev, width = tokens.shape[2:]
    scale = 1.0 / math.sqrt(width)
    grad_scale = scale / (tok_dev * NS)
    parts = []
    for s in range(2):
        x = tokens[0, s]
        gram = jnp.einsum("td,te->de", x, x, preferred_element_type=F32).astype(BF16)
        cross = jnp.einsum("tfk,td->fkd", targets[0, s], x, preferred_element_type=F32).astype(BF16)
        gram = jnp.moveaxis(gram.reshape(NZ, NK, 32, width), 1, 0)
        parts.append(jnp.concatenate([cross.reshape(2, NZ, 64, width), gram], axis=2))
    part = jnp.stack(parts)
    vmem = pl.BlockSpec(memory_space=pltpu.VMEM)
    smem = pl.BlockSpec(memory_space=pltpu.SMEM)
    dma = pltpu.SemaphoreType.DMA
    D = width
    new_outer, new_inner = pl.pallas_call(
        functools.partial(kernel, n_rep, scale, grad_scale),
        name="window",
        out_shape=(
            jax.ShapeDtypeStruct((2, 16, D), F32),
            jax.ShapeDtypeStruct((2, 16, D), F32),
        ),
        in_specs=[smem, smem] + [vmem] * 6,
        out_specs=(vmem, vmem),
        scratch_shapes=[
            pltpu.VMEM((2, NZ, ROWS, D), BF16),
            pltpu.VMEM((2, 2, 7, HALF, D), BF16),
            pltpu.VMEM((2, 2, 7, HALF, D), BF16),
            pltpu.VMEM((2, ROWS, D), F32),
            pltpu.VMEM((2, 64, D), BF16),
            pltpu.VMEM((2, 64, D), BF16),
            pltpu.VMEM((2, 32, D), F32),
            pltpu.VMEM((2, 16, D), BF16),
            pltpu.VMEM((2, 16, D), BF16),
            pltpu.VMEM((2, 2, 16, D), F32),
            pltpu.VMEM((2, NZ, NK, 32, D), BF16),
            pltpu.VMEM((2, 1, 128), F32),
            pltpu.VMEM((2, NS, 1, 128), F32),
            pltpu.VMEM((2, n_rep, 1, D), F32),
            pltpu.VMEM((2, n_rep, 1, D), F32),
            pltpu.VMEM((2, n_rep, 1, D), F32),
            dma((2,)),
            dma((2,)),
            dma((2, 2, 7)),
            dma((2, 2, 7)),
            dma((2,)),
            dma((2,)),
            dma((2,)),
            dma((2,)),
            dma((2, NZ)),
            dma((2, NZ)),
            dma((2, NZ)),
            dma((2, NZ)),
            dma((2, NS)),
            dma((2, NS)),
            dma((2, n_rep)),
            dma((2, n_rep)),
            dma((2, n_rep)),
            dma((2, n_rep)),
        ],
        compiler_params=pltpu.CompilerParams(collective_id=0, has_side_effects=True),
    )(
        step_count,
        first_fragment,
        part,
        inner_weights[0],
        first_moment[0],
        second_moment[0],
        outer_weights,
        outer_velocity,
    )
    return new_outer, new_inner[None]


def solution(mesh):
    in_specs = (
        P("rep", None, "shard", None),
        P("rep", None, "shard", None),
        P("rep", None, "shard", None),
        P(None, "shard", None),
        P(None, "shard", None),
        P("rep", None, "shard", None),
        P("rep", None, "shard", None, None),
        P(),
        P(),
    )
    out_specs = (P(None, "shard", None), P("rep", None, "shard", None))
    return jax.shard_map(body, mesh=mesh, in_specs=in_specs, out_specs=out_specs, check_vma=False)
```

```python
import functools
import math

import jax
import jax.numpy as jnp
from jax import lax
from jax.experimental import pallas as pl
from jax.experimental.pallas import tpu as pltpu
from jax.sharding import PartitionSpec as P

beta_one = 0.9
beta_two = 0.95
inner_rate = 0.1
adam_eps = 1e-08
decay_rate = 0.1
clip_norm = 0.02
outer_rate = 0.7
outer_momentum = 0.9
mixing = 0.5

NZ, NY, NK = 8, 2, 2
NS = NZ * NY * NK
MESH = pl.DeviceIdType.MESH
F32, BF16 = jnp.float32, jnp.bfloat16


class Ring:
    def __init__(self, dev, mine, other, out, got, ss, rs, half, sub):
        self.dev, self.mine, self.other = dev, mine, other
        self.out, self.got, self.ss, self.rs = out, got, ss, rs
        self.half, self.sub = half, sub

    def copy(self, d, i, u):
        z, y, k, at, remote = self.dev
        zz = (z + 1) % NZ if d == 0 else (z + NZ - 1) % NZ
        rows = pl.ds(u * self.sub, self.sub)
        return remote(
            self.out.at[d, i, rows], self.got.at[d, i, rows], self.ss.at[d, i, u], self.rs.at[d, i, u], at(zz, y, k)
        )

    def own(self, owner, h, u):
        k = self.dev[2]
        rows = pl.ds(self.half * h + u * self.sub, self.sub)
        return self.mine[k, owner, rows, :].astype(F32) + self.other[owner, rows, :].astype(F32)

    def arrived(self, d, i, u):
        self.copy(d, i, u).wait_recv()
        return self.got[d, i, pl.ds(u * self.sub, self.sub), :].astype(F32)

    def step(self, t):
        z = self.dev[0]
        for long in (True, False):
            if not long and t == 3:
                continue
            hops = 4 if long else 3
            i = t if long else 4 + t
            for u in range(self.half // self.sub):
                for d in range(2):
                    h = d if long else 1 - d
                    owner = (z + hops - t) % NZ if d == 0 else (z + NZ - hops + t) % NZ
                    val = self.own(owner, h, u)
                    if t > 0:
                        val = val + self.arrived(d, i - 1, u)
                    self.out[d, i, pl.ds(u * self.sub, self.sub), :] = val.astype(BF16)
                    self.copy(d, i, u).start()

    def finish(self, total):
        z = self.dev[0]
        for u in range(self.half // self.sub):
            for h in range(2):
                val = self.own(z, h, u) + self.arrived(1 - h, 6, u) + self.arrived(h, 3, u)
                total[pl.ds(self.half * h + u * self.sub, self.sub), :] = val

    def drain(self):
        for d in range(2):
            for i in range(7):
                for u in range(self.half // self.sub):
                    self.copy(d, i, u).wait_send()


def kernel(n_rep, scale, grad_scale, count_ref, first_ref, x_hbm, t_hbm, w_ref, m_ref, v_ref, outer_ref, vel_ref, out_ref, *scratch):
    names, shapes = zip(*scratch_of(n_rep))
    r = dict(zip(names, scratch, strict=True))
    rep = lax.axis_index("rep")
    me = lax.axis_index("shard")
    z = me // 4
    y = (me // 2) % 2
    k = me % 2
    q = z * 2 + k

    def at(zz, yy, kk):
        return (rep, zz * 4 + yy * 2 + kk)

    def plane(qq):
        return at(qq // 2, y, qq % 2)

    partner = at(z, y, 1 - k)
    across = at(z, 1 - y, k)

    def remote(src, dst, ss, rs, dev):
        return pltpu.make_async_remote_copy(
            src_ref=src, dst_ref=dst, send_sem=ss, recv_sem=rs, device_id=dev, device_id_type=MESH
        )

    barrier = pltpu.get_barrier_semaphore()

    @pl.loop(1, NS)
    def _(o):
        pl.semaphore_signal(barrier, inc=1, device_id=(rep, (me + o) % NS), device_id_type=MESH)

    @pl.loop(1, n_rep)
    def _(o):
        pl.semaphore_signal(barrier, inc=1, device_id=((rep + o) % n_rep, me), device_id_type=MESH)

    def load(s):
        return (
            pltpu.make_async_copy(x_hbm.at[s], r["x"].at[s], r["load"].at[s, 0]),
            pltpu.make_async_copy(t_hbm.at[s], r["t"].at[s], r["load"].at[s, 1]),
        )

    for s in range(2):
        for c in load(s):
            c.start()

    rep_out, rep_in, rep_all = r["rep_out"], r["rep_in"], r["rep_all"]

    def rep_send_copy(s, o):
        to = (rep + o) % n_rep
        return remote(rep_out.at[s, to], rep_in.at[s, o], r["rs_s"].at[s, o], r["rs_r"].at[s, o], (to, me))

    def rep_back_copy(s, o, row):
        to = (rep + o) % n_rep
        return remote(rep_all.at[s, row], rep_all.at[s, row], r["ra_s"].at[s, o], r["ra_r"].at[s, o], (to, me))

    def rep_start(s, value):
        rep_out[s] = value.reshape(n_rep, 1, value.shape[-1])

        @pl.loop(1, n_rep)
        def _(o):
            rep_send_copy(s, o).start()

    def rep_middle(s):
        @pl.loop(1, n_rep)
        def _(o):
            rep_send_copy(s, o).wait_recv()

        acc = rep_out[s, rep]
        for o in range(1, n_rep):
            acc = acc + rep_in[s, o]
        rep_all[s, rep] = acc

        @pl.loop(1, n_rep)
        def _(o):
            rep_back_copy(s, o, rep).start()

    def rep_end(s):
        @pl.loop(1, n_rep)
        def _(o):
            rep_back_copy(s, o, (rep + n_rep - o) % n_rep).wait_recv()

        return rep_all[s].reshape(n_rep, rep_all.shape[-1])

    def core_a():
        return remote(r["pa"].at[1 - k], r["ca"], r["core_s"].at[0], r["core_r"].at[0], partner)

    def core_b():
        return remote(r["pb"].at[1 - k], r["cb"], r["core_s"].at[1], r["core_r"].at[1], partner)

    dev = (z, y, k, at, remote)
    ring_a = Ring(dev, r["pa"], r["ca"], r["ra_out"], r["ra_in"], r["ring_a_s"], r["ring_a_r"], 64, SUB_A)
    ring_b = Ring(dev, r["pb"], r["cb"], r["rb_out"], r["rb_in"], r["ring_b_s"], r["ring_b_r"], 32, SUB_B)

    def tdot(a, b):
        return lax.dot_general(a, b, (((0,), (0,)), ((), ())), preferred_element_type=F32)

    def gram_rows(s, first_row):
        x = r["x"][s]
        g = tdot(x, x).astype(BF16).reshape(NZ, NK, 32, 512)
        for kk in range(NK):
            r["pa"][kk, :, pl.ds(first_row, 32), :] = g[:, kk]

    for c in load(0):
        c.wait()
    gram_rows(0, 64)
    flat = r["t"][0].reshape(512, 1024)
    for kk in range(NK):
        ct = tdot(r["x"][0], flat[:, 512 * kk : 512 * kk + 512])
        r["pa"][kk, :, pl.ds(0, 64), :] = ct.astype(BF16).reshape(NZ, 64, 512)
    for c in load(1):
        c.wait()
    gram_rows(1, 96)
    w, m, v = w_ref[...], m_ref[...], v_ref[...]
    r["wb"][...] = w.astype(BF16)
    r["wall"][z, k] = r["wb"][k]

    pl.semaphore_wait(barrier, NS - 1 + n_rep - 1)
    core_a().start()

    def w_swap():
        return remote(r["wb"].at[1 - k], r["wall"].at[z, k], r["wsw_s"], r["wsw_r"], partner)

    def w_copy(d, t, block):
        zz = (z + 1) % NZ if d == 0 else (z + NZ - 1) % NZ
        return remote(r["wall"].at[block], r["wall"].at[block], r["w_s"].at[d, t], r["w_r"].at[d, t], at(zz, y, k))

    def w_step(t):
        if t == 0:
            remote(r["wb"].at[k], r["wall"].at[z, 1 - k], r["wsw_s"], r["wsw_r"], partner).wait_recv()
        for d in range(2 if t < 3 else 1):
            block = (z + NZ - t) % NZ if d == 0 else (z + t) % NZ
            if t > 0:
                w_copy(d, t - 1, block).wait_recv()
            w_copy(d, t, block).start()

    w_swap().start()
    lead = first_ref[0] == 0
    rep_start(0, jnp.where(lead, w[0], w[1]))

    flat = r["t"][1].reshape(512, 1024)
    for kk in range(NK):
        c1 = tdot(flat[:, 512 * kk : 512 * kk + 512], r["x"][1])
        r["pb"][kk] = c1.astype(BF16).reshape(NZ, 64, 512)
    core_b().start()
    row = lax.broadcasted_iota(jnp.int32, (512, 256), 0)
    col = lax.broadcasted_iota(jnp.int32, (512, 256), 1)
    place = jnp.where((row // 64 == col // 32) & (row % 32 == col % 32), (row // 32) % 2, 2)
    pick_mine = jnp.where(place == y, 1.0, 0.0).astype(BF16)
    pick_other = jnp.where(place == 1 - y, 1.0, 0.0).astype(BF16)

    core_a().wait_recv()
    for t in range(4):
        ring_a.step(t)
        w_step(t)

    def y_copy(i):
        name = ("yc", "yg0", "yg1")[i]
        return remote(r[name + "_out"], r[name + "_in"], r["y_s"].at[i], r["y_r"].at[i], across)

    ring_a.finish(r["ta"])
    hi = r["ta"][pl.ds(0, 64), :].astype(BF16)
    lo = (r["ta"][pl.ds(0, 64), :] - hi.astype(F32)).astype(BF16)
    r["yc_out"][...] = jnp.dot(hi, pick_other, preferred_element_type=F32).astype(BF16)
    y_copy(0).start()
    r["yg0_out"][...] = r["ta"][pl.ds(64, 32), :].astype(BF16)
    y_copy(1).start()
    r["yg1_out"][...] = r["ta"][pl.ds(96, 32), :].astype(BF16)
    y_copy(2).start()
    rep_middle(0)
    core_b().wait_recv()
    ring_b.step(0)
    cross = jnp.dot(hi, pick_mine, preferred_element_type=F32) + jnp.dot(lo, pick_mine, preferred_element_type=F32)
    w_copy(0, 3, (z + NZ - 4) % NZ).wait_recv()
    w_copy(1, 2, (z + 3) % NZ).wait_recv()

    def g0_swap(kk):
        return remote(r["gcol"].at[kk], r["gcol"].at[kk], r["gsw_s"], r["gsw_r"], partner)

    y_copy(0).wait_recv()
    cross = cross + r["yc_in"][...].astype(F32)
    y_copy(1).wait_recv()
    r["gcol"][k] = (r["ta"][pl.ds(64, 32), :] + r["yg0_in"][...].astype(F32)).astype(BF16)
    g0_swap(k).start()

    def ag_copy(o, src):
        return remote(
            r["gram"].at[src, k], r["gram"].at[src, k], r["ag_s"].at[o], r["ag_r"].at[o], at((z + o) % NZ, y, k)
        )

    def fw_copy(o, kk):
        src = (z + NZ - o) % NZ
        return remote(r["gram"].at[src, kk], r["gram"].at[src, kk], r["fw_s"].at[o], r["fw_r"].at[o], partner)

    y_copy(2).wait_recv()
    r["gram"][z, k] = (r["ta"][pl.ds(96, 32), :] + r["yg1_in"][...].astype(F32)).astype(BF16)

    def a_copy(o):
        to = (q + o) % 16
        return remote(r["gout"].at[to], r["gin"].at[k, z], r["a_s"].at[o], r["a_r"].at[o], plane(to))

    def a_from(o):
        src = (q + 16 - o) % 16
        return remote(r["gout"].at[q], r["gin"].at[src % 2, src // 2], r["a_s"].at[o], r["a_r"].at[o], plane(src))

    def n_copy(s, o):
        return remote(r["n_out"].at[s], r["n_in"].at[s, o], r["n_s"].at[s, o], r["n_r"].at[s, o], (rep, (me + o) % NS))

    def norm_start(s, g):
        total = jnp.sum(jnp.sum(g * g, axis=0, keepdims=True), axis=1, keepdims=True)
        r["n_out"][s] = jnp.broadcast_to(total, (1, 128))

        @pl.loop(1, NS)
        def _(o):
            n_copy(s, o).start()

    def clip_factor(s):
        @pl.loop(1, NS)
        def _(o):
            n_copy(s, o).wait_recv()

        acc = r["n_out"][s]
        for o in range(1, NS):
            acc = acc + r["n_in"][s, o]
        f = jnp.minimum(1.0, clip_norm / (jnp.sqrt(acc) + 1e-06))
        return f[:, :1].reshape(1, 1, 1)

    def ndot(a, b):
        return lax.dot_general(a, b, (((1,), (1,)), ((), ())), preferred_element_type=F32)

    g0_swap(1 - k).wait_recv()
    gt = ndot(r["gcol"][...].reshape(64, 512), r["wall"][...].reshape(256, 512))
    gt = (gt * scale - cross) * grad_scale
    norm_start(0, gt)
    r["gout"][...] = gt.T.astype(BF16).reshape(16, 16, 64)
    r["gin"][k, z] = r["gout"][q]

    @pl.loop(1, 16)
    def _(o):
        a_copy(o).start()

    for o in (4, 3, 5, 2, 6, 1, 7):
        ag_copy(o, z).start()
    fw_copy(0, k).start()
    ring_b.step(1)
    ring_b.step(2)
    for o in (1, 7, 2, 6):
        ag_copy(o, (z + NZ - o) % NZ).wait_recv()
        fw_copy(o, k).start()
    ring_b.step(3)
    for o in (3, 5, 4):
        ag_copy(o, (z + NZ - o) % NZ).wait_recv()
        fw_copy(o, k).start()

    ring_b.finish(r["tb"])
    peers = ((0, 1 - k), (1, k), (1, 1 - k))

    def c_copy(i):
        dy, kk = peers[i]
        yy = y if dy == 0 else 1 - y
        return remote(r["c_out"].at[i], r["c_in"].at[i], r["c_s"].at[i], r["c_r"].at[i], at(z, yy, kk))

    for i in (2, 1, 0):
        dy, kk = peers[i]
        yy = y if dy == 0 else 1 - y
        r["c_out"][i] = r["tb"][pl.ds(yy * 32 + kk * 16, 16), :].astype(BF16)
        c_copy(i).start()

    def adam(s, w, m, v, clipped):
        count = jnp.full((1, 8, 128), count_ref[0].astype(F32) + s, F32)
        one = (1.0 - jnp.exp(count * math.log(beta_one)))[:, :1, :1]
        two = (1.0 - jnp.exp(count * math.log(beta_two)))[:, :1, :1]
        m = beta_one * m + (1.0 - beta_one) * clipped
        v = beta_two * v + (1.0 - beta_two) * clipped * clipped
        update = m / one / (jnp.sqrt(v / two) + adam_eps)
        return w - inner_rate * (update + decay_rate * w), m, v

    def outer_step(theta, speed, weight_sum):
        delta = theta - weight_sum * (1.0 / n_rep)
        speed = outer_momentum * speed + delta
        return theta - outer_rate * (outer_momentum * speed + delta)

    theta0 = outer_step(
        jnp.where(lead, outer_ref[0], outer_ref[1]), jnp.where(lead, vel_ref[0], vel_ref[1]), rep_end(0)
    )

    @pl.loop(1, 16)
    def _(o):
        a_from(o).wait_recv()

    for zz in range(NZ):
        for f in range(2):
            r["g0"][f, :, 64 * zz : 64 * zz + 64] = r["gin"][f, zz].astype(F32)
    clipped = r["g0"][...] * clip_factor(0)
    w, m, v = adam(0, w, m, v, clipped)
    rep_start(1, jnp.where(lead, w[1], w[0]))
    a = jnp.where(lead, mixing * theta0 + (1.0 - mixing) * w[0], w[0])
    b = jnp.where(lead, w[1], mixing * theta0 + (1.0 - mixing) * w[1])
    w = jnp.stack([a, b])
    for o in range(NZ):
        fw_copy(o, 1 - k).wait_recv()
    prod = jnp.dot(w.reshape(32, 512).astype(BF16), r["gram"][...].reshape(512, 512), preferred_element_type=F32)
    for i in range(3):
        c_copy(i).wait_recv()
    r["c1"][k] = r["tb"][pl.ds(y * 32 + k * 16, 16), :] + r["c_in"][1].astype(F32)
    r["c1"][1 - k] = r["c_in"][0].astype(F32) + r["c_in"][2].astype(F32)
    g = (prod * scale - r["c1"][...].reshape(32, 512)) * grad_scale
    norm_start(1, g)
    rep_middle(1)
    clipped = g.reshape(2, 16, 512) * clip_factor(1)
    w, m, v = adam(1, w, m, v, clipped)
    theta1 = outer_step(
        jnp.where(lead, outer_ref[1], outer_ref[0]), jnp.where(lead, vel_ref[1], vel_ref[0]), rep_end(1)
    )
    out_ref[0] = jnp.where(lead, theta0, theta1)
    out_ref[1] = jnp.where(lead, theta1, theta0)
    out_ref[2] = jnp.where(lead, w[0], mixing * theta1 + (1.0 - mixing) * w[0])
    out_ref[3] = jnp.where(lead, mixing * theta1 + (1.0 - mixing) * w[1], w[1])

    core_a().wait_send()
    core_b().wait_send()
    ring_a.drain()
    ring_b.drain()
    w_swap().wait_send()
    for t in range(4):
        for d in range(2 if t < 3 else 1):
            w_copy(d, t, (z + NZ - t) % NZ if d == 0 else (z + t) % NZ).wait_send()
    for i in range(3):
        y_copy(i).wait_send()
        c_copy(i).wait_send()
    g0_swap(k).wait_send()
    for o in range(1, NZ):
        ag_copy(o, z).wait_send()
    for o in range(NZ):
        fw_copy(o, k).wait_send()

    @pl.loop(1, 16)
    def _(o):
        a_copy(o).wait_send()

    for s in range(2):

        @pl.loop(1, NS)
        def _(o):
            n_copy(s, o).wait_send()

        @pl.loop(1, n_rep)
        def _(o):
            rep_send_copy(s, o).wait_send()
            rep_back_copy(s, o, rep).wait_send()


SUB_A, SUB_B = 32, 32


def scratch_of(n_rep):
    vmem, dma = pltpu.VMEM, pltpu.SemaphoreType.DMA
    D = 512
    return (
        ("x", vmem((2, 512, D), BF16)),
        ("t", vmem((2, 512, 2, D), BF16)),
        ("pa", vmem((NK, NZ, 128, D), BF16)),
        ("pb", vmem((NK, NZ, 64, D), BF16)),
        ("ca", vmem((NZ, 128, D), BF16)),
        ("cb", vmem((NZ, 64, D), BF16)),
        ("ra_out", vmem((2, 7, 64, D), BF16)),
        ("ra_in", vmem((2, 7, 64, D), BF16)),
        ("rb_out", vmem((2, 7, 32, D), BF16)),
        ("rb_in", vmem((2, 7, 32, D), BF16)),
        ("ta", vmem((128, D), F32)),
        ("tb", vmem((64, D), F32)),
        ("wb", vmem((2, 16, D), BF16)),
        ("wall", vmem((NZ, NK, 16, D), BF16)),
        ("yc_out", vmem((64, 256), BF16)),
        ("yc_in", vmem((64, 256), BF16)),
        ("yg0_out", vmem((32, D), BF16)),
        ("yg0_in", vmem((32, D), BF16)),
        ("yg1_out", vmem((32, D), BF16)),
        ("yg1_in", vmem((32, D), BF16)),
        ("gcol", vmem((NK, 32, D), BF16)),
        ("gram", vmem((NZ, NK, 32, D), BF16)),
        ("gout", vmem((16, 16, 64), BF16)),
        ("gin", vmem((2, NZ, 16, 64), BF16)),
        ("g0", vmem((2, 16, D), F32)),
        ("c_out", vmem((3, 16, D), BF16)),
        ("c_in", vmem((3, 16, D), BF16)),
        ("c1", vmem((2, 16, D), F32)),
        ("n_out", vmem((2, 1, 128), F32)),
        ("n_in", vmem((2, NS, 1, 128), F32)),
        ("rep_out", vmem((2, n_rep, 1, D), F32)),
        ("rep_in", vmem((2, n_rep, 1, D), F32)),
        ("rep_all", vmem((2, n_rep, 1, D), F32)),
        ("load", dma((2, 2))),
        ("core_s", dma((2,))),
        ("core_r", dma((2,))),
        ("ring_a_s", dma((2, 7, 64 // SUB_A))),
        ("ring_a_r", dma((2, 7, 64 // SUB_A))),
        ("ring_b_s", dma((2, 7, 32 // SUB_B))),
        ("ring_b_r", dma((2, 7, 32 // SUB_B))),
        ("wsw_s", dma),
        ("wsw_r", dma),
        ("w_s", dma((2, 4))),
        ("w_r", dma((2, 4))),
        ("y_s", dma((3,))),
        ("y_r", dma((3,))),
        ("gsw_s", dma),
        ("gsw_r", dma),
        ("ag_s", dma((NZ,))),
        ("ag_r", dma((NZ,))),
        ("fw_s", dma((NZ,))),
        ("fw_r", dma((NZ,))),
        ("a_s", dma((16,))),
        ("a_r", dma((16,))),
        ("c_s", dma((3,))),
        ("c_r", dma((3,))),
        ("n_s", dma((2, NS))),
        ("n_r", dma((2, NS))),
        ("rs_s", dma((2, n_rep))),
        ("rs_r", dma((2, n_rep))),
        ("ra_s", dma((2, n_rep))),
        ("ra_r", dma((2, n_rep))),
    )


def body(
    inner_weights,
    first_moment,
    second_moment,
    outer_weights,
    outer_velocity,
    tokens,
    targets,
    step_count,
    first_fragment,
):
    n_rep = lax.axis_size("rep")
    tok_dev, width = tokens.shape[2:]
    scale = 1.0 / math.sqrt(width)
    grad_scale = scale / (tok_dev * NS)
    vmem = pl.BlockSpec(memory_space=pltpu.VMEM)
    smem = pl.BlockSpec(memory_space=pltpu.SMEM)
    anywhere = pl.BlockSpec(memory_space=pl.ANY)
    out = pl.pallas_call(
        functools.partial(kernel, n_rep, scale, grad_scale),
        name="window",
        out_shape=jax.ShapeDtypeStruct((4, 16, width), F32),
        in_specs=[smem, smem, anywhere, anywhere] + [vmem] * 5,
        out_specs=vmem,
        scratch_shapes=[shape for _, shape in scratch_of(n_rep)],
        compiler_params=pltpu.CompilerParams(collective_id=0, has_side_effects=True),
    )(
        step_count,
        first_fragment,
        tokens[0],
        targets[0],
        inner_weights[0],
        first_moment[0],
        second_moment[0],
        outer_weights,
        outer_velocity,
    )
    return out[:2], out[2:][None]


def solution(mesh):
    in_specs = (
        P("rep", None, "shard", None),
        P("rep", None, "shard", None),
        P("rep", None, "shard", None),
        P(None, "shard", None),
        P(None, "shard", None),
        P("rep", None, "shard", None),
        P("rep", None, "shard", None, None),
        P(),
        P(),
    )
    out_specs = (P(None, "shard", None), P("rep", None, "shard", None))
    return jax.shard_map(body, mesh=mesh, in_specs=in_specs, out_specs=out_specs, check_vma=False)
```

```python
import functools
import math

import jax
import jax.numpy as jnp
from jax import lax
from jax.experimental import pallas as pl
from jax.experimental.pallas import tpu as pltpu
from jax.sharding import PartitionSpec as P

beta_one = 0.9
beta_two = 0.95
inner_rate = 0.1
adam_eps = 1e-08
decay_rate = 0.1
clip_norm = 0.02
outer_rate = 0.7
outer_momentum = 0.9
mixing = 0.5

NZ, NY, NK = 8, 2, 2
NS = NZ * NY * NK
MESH = pl.DeviceIdType.MESH
F32, BF16 = jnp.float32, jnp.bfloat16


class Ring:
    def __init__(self, dev, mine, other, out, got, ss, rs, half, sub):
        self.dev, self.mine, self.other = dev, mine, other
        self.out, self.got, self.ss, self.rs = out, got, ss, rs
        self.half, self.sub = half, sub

    def copy(self, d, i, u):
        z, y, k, at, remote = self.dev
        zz = (z + 1) % NZ if d == 0 else (z + NZ - 1) % NZ
        rows = pl.ds(u * self.sub, self.sub)
        return remote(
            self.out.at[d, i, rows], self.got.at[d, i, rows], self.ss.at[d, i, u], self.rs.at[d, i, u], at(zz, y, k)
        )

    def own(self, owner, h, u):
        k = self.dev[2]
        rows = pl.ds(self.half * h + u * self.sub, self.sub)
        return self.mine[k, owner, rows, :].astype(F32) + self.other[owner, rows, :].astype(F32)

    def arrived(self, d, i, u):
        self.copy(d, i, u).wait_recv()
        return self.got[d, i, pl.ds(u * self.sub, self.sub), :].astype(F32)

    def step(self, t):
        z = self.dev[0]
        for long in (True, False):
            if not long and t == 3:
                continue
            hops = 4 if long else 3
            i = t if long else 4 + t
            for u in range(self.half // self.sub):
                for d in range(2):
                    h = d if long else 1 - d
                    owner = (z + hops - t) % NZ if d == 0 else (z + NZ - hops + t) % NZ
                    val = self.own(owner, h, u)
                    if t > 0:
                        val = val + self.arrived(d, i - 1, u)
                    self.out[d, i, pl.ds(u * self.sub, self.sub), :] = val.astype(BF16)
                    self.copy(d, i, u).start()

    def finish(self, total):
        z = self.dev[0]
        for u in range(self.half // self.sub):
            for h in range(2):
                val = self.own(z, h, u) + self.arrived(1 - h, 6, u) + self.arrived(h, 3, u)
                total[pl.ds(self.half * h + u * self.sub, self.sub), :] = val

    def drain(self):
        for d in range(2):
            for i in range(7):
                for u in range(self.half // self.sub):
                    self.copy(d, i, u).wait_send()


def kernel(n_rep, scale, grad_scale, count_ref, first_ref, x_hbm, t_hbm, w_hbm, m_hbm, v_hbm, outer_hbm, vel_hbm, out_ref, *scratch):
    names, shapes = zip(*scratch_of(n_rep))
    r = dict(zip(names, scratch, strict=True))
    state = (w_hbm, m_hbm, v_hbm, outer_hbm, vel_hbm)
    w_ref, m_ref, v_ref, outer_ref, vel_ref = (r["state"].at[i] for i in range(5))
    rep = lax.axis_index("rep")
    me = lax.axis_index("shard")
    z = me // 4
    y = (me // 2) % 2
    k = me % 2
    q = z * 2 + k

    def at(zz, yy, kk):
        return (rep, zz * 4 + yy * 2 + kk)

    def plane(qq):
        return at(qq // 2, y, qq % 2)

    partner = at(z, y, 1 - k)
    across = at(z, 1 - y, k)

    def remote(src, dst, ss, rs, dev):
        return pltpu.make_async_remote_copy(
            src_ref=src, dst_ref=dst, send_sem=ss, recv_sem=rs, device_id=dev, device_id_type=MESH
        )

    barrier = pltpu.get_barrier_semaphore()

    for dev in (partner, at((z + 1) % NZ, y, k), at((z + NZ - 1) % NZ, y, k), across):
        pl.semaphore_signal(barrier, inc=1, device_id=dev, device_id_type=MESH)

    @pl.loop(1, n_rep)
    def _(o):
        pl.semaphore_signal(barrier, inc=1, device_id=((rep + o) % n_rep, me), device_id_type=MESH)

    def load(s):
        return (
            pltpu.make_async_copy(x_hbm.at[s], r["x"].at[s], r["load"].at[s, 0]),
            pltpu.make_async_copy(t_hbm.at[s], r["t"].at[s], r["load"].at[s, 1]),
        )

    def load_state(i):
        return pltpu.make_async_copy(state[i], r["state"].at[i], r["load_state"].at[i])

    for c in load(0):
        c.start()
    for i in range(5):
        load_state(i).start()

    rep_out, rep_in, rep_all = r["rep_out"], r["rep_in"], r["rep_all"]

    def rep_send_copy(s, o):
        to = (rep + o) % n_rep
        return remote(rep_out.at[s, to], rep_in.at[s, o], r["rs_s"].at[s, o], r["rs_r"].at[s, o], (to, me))

    def rep_back_copy(s, o, row):
        to = (rep + o) % n_rep
        return remote(rep_all.at[s, row], rep_all.at[s, row], r["ra_s"].at[s, o], r["ra_r"].at[s, o], (to, me))

    def rep_start(s, value):
        rep_out[s] = value.reshape(n_rep, 1, value.shape[-1])

        @pl.loop(1, n_rep)
        def _(o):
            rep_send_copy(s, o).start()

    def rep_middle(s):
        @pl.loop(1, n_rep)
        def _(o):
            rep_send_copy(s, o).wait_recv()

        acc = rep_out[s, rep]
        for o in range(1, n_rep):
            acc = acc + rep_in[s, o]
        rep_all[s, rep] = acc

        @pl.loop(1, n_rep)
        def _(o):
            rep_back_copy(s, o, rep).start()

    def rep_end(s):
        @pl.loop(1, n_rep)
        def _(o):
            rep_back_copy(s, o, (rep + n_rep - o) % n_rep).wait_recv()

        return rep_all[s].reshape(n_rep, rep_all.shape[-1])

    def core_a():
        return remote(r["pa"].at[1 - k], r["ca"], r["core_s"].at[0], r["core_r"].at[0], partner)

    def core_b():
        return remote(r["pb"].at[1 - k], r["cb"], r["core_s"].at[1], r["core_r"].at[1], partner)

    dev = (z, y, k, at, remote)
    ring_a = Ring(dev, r["pa"], r["ca"], r["ra_out"], r["ra_in"], r["ring_a_s"], r["ring_a_r"], 64, SUB_A)
    ring_b = Ring(dev, r["pb"], r["cb"], r["rb_out"], r["rb_in"], r["ring_b_s"], r["ring_b_r"], 32, SUB_B)

    def tdot(a, b):
        return lax.dot_general(a, b, (((0,), (0,)), ((), ())), preferred_element_type=F32)

    def gram_rows(s, first_row):
        x = r["x"][s]
        xt = x.T
        g = jnp.dot(xt, x, preferred_element_type=F32).astype(BF16).reshape(NZ, NK, 32, 512)
        for kk in range(NK):
            r["pa"][kk, :, pl.ds(first_row, 32), :] = g[:, kk]
        return xt

    load(0)[0].wait()
    xt = gram_rows(0, 64)
    load(0)[1].wait()
    for c in load(1):
        c.start()
    flat = r["t"][0].reshape(512, 1024)
    for kk in range(NK):
        ct = jnp.dot(xt, flat[:, 512 * kk : 512 * kk + 512], preferred_element_type=F32)
        r["pa"][kk, :, pl.ds(0, 64), :] = ct.astype(BF16).reshape(NZ, 64, 512)
    for i in range(5):
        load_state(i).wait()
    w, m, v = w_ref[...], m_ref[...], v_ref[...]
    r["wb"][...] = w.astype(BF16)
    r["wall"][z, k] = r["wb"][k]
    for c in load(1):
        c.wait()
    gram_rows(1, 96)

    pl.semaphore_wait(barrier, 4 + n_rep - 1)
    core_a().start()

    def w_swap():
        return remote(r["wb"].at[1 - k], r["wall"].at[z, k], r["wsw_s"], r["wsw_r"], partner)

    def w_copy(d, t, block):
        zz = (z + 1) % NZ if d == 0 else (z + NZ - 1) % NZ
        return remote(r["wall"].at[block], r["wall"].at[block], r["w_s"].at[d, t], r["w_r"].at[d, t], at(zz, y, k))

    def w_step(t):
        if t == 0:
            remote(r["wb"].at[k], r["wall"].at[z, 1 - k], r["wsw_s"], r["wsw_r"], partner).wait_recv()
        for d in range(2 if t < 3 else 1):
            block = (z + NZ - t) % NZ if d == 0 else (z + t) % NZ
            if t > 0:
                w_copy(d, t - 1, block).wait_recv()
            w_copy(d, t, block).start()

    w_swap().start()
    lead = first_ref[0] == 0

    w_step(0)
    core_a().wait_recv()
    ring_a.step(0)
    w_step(1)
    flat = r["t"][1].reshape(512, 1024)
    for kk in range(NK):
        r["pb"][kk] = tdot(flat[:, 512 * kk : 512 * kk + 512], r["x"][1]).astype(BF16).reshape(NZ, 64, 512)
    core_b().start()
    ring_a.step(1)
    w_step(2)
    rep_start(0, jnp.where(lead, w[0], w[1]))
    ring_a.step(2)
    w_step(3)
    row = lax.broadcasted_iota(jnp.int32, (512, 256), 0)
    col = lax.broadcasted_iota(jnp.int32, (512, 256), 1)
    place = jnp.where((row // 64 == col // 32) & (row % 32 == col % 32), (row // 32) % 2, 2)
    pick_mine = jnp.where(place == y, 1.0, 0.0).astype(BF16)
    pick_other = jnp.where(place == 1 - y, 1.0, 0.0).astype(BF16)

    ring_a.step(3)
    core_b().wait_recv()
    ring_b.step(0)

    def y_copy(i):
        name = ("yc", "yg0", "yg1")[i]
        return remote(r[name + "_out"], r[name + "_in"], r["y_s"].at[i], r["y_r"].at[i], across)

    ring_a.finish(r["ta"])
    hi = r["ta"][pl.ds(0, 64), :].astype(BF16)
    lo = (r["ta"][pl.ds(0, 64), :] - hi.astype(F32)).astype(BF16)
    r["yc_out"][...] = jnp.dot(hi, pick_other, preferred_element_type=F32).astype(BF16)
    y_copy(0).start()
    r["yg0_out"][...] = r["ta"][pl.ds(64, 32), :].astype(BF16)
    y_copy(1).start()
    r["yg1_out"][...] = r["ta"][pl.ds(96, 32), :].astype(BF16)
    y_copy(2).start()
    ring_b.step(1)
    rep_middle(0)
    cross = jnp.dot(hi, pick_mine, preferred_element_type=F32) + jnp.dot(lo, pick_mine, preferred_element_type=F32)
    w_copy(0, 3, (z + NZ - 4) % NZ).wait_recv()
    w_copy(1, 2, (z + 3) % NZ).wait_recv()

    ring_b.step(2)

    def g0_swap(kk):
        return remote(r["gcol"].at[kk], r["gcol"].at[kk], r["gsw_s"], r["gsw_r"], partner)

    y_copy(0).wait_recv()
    cross = cross + r["yc_in"][...].astype(F32)
    y_copy(1).wait_recv()
    r["gcol"][k] = (r["ta"][pl.ds(64, 32), :] + r["yg0_in"][...].astype(F32)).astype(BF16)
    g0_swap(k).start()
    ring_b.step(3)

    def ag_copy(o, src):
        return remote(
            r["gram"].at[src, k], r["gram"].at[src, k], r["ag_s"].at[o], r["ag_r"].at[o], at((z + o) % NZ, y, k)
        )

    def fw_copy(o, kk):
        src = (z + NZ - o) % NZ
        return remote(r["gram"].at[src, kk], r["gram"].at[src, kk], r["fw_s"].at[o], r["fw_r"].at[o], partner)

    y_copy(2).wait_recv()
    r["gram"][z, k] = (r["ta"][pl.ds(96, 32), :] + r["yg1_in"][...].astype(F32)).astype(BF16)


    for o in (4, 3, 5, 2, 6, 1, 7):
        ag_copy(o, z).start()
    fw_copy(0, k).start()

    def a_copy(o):
        to = (q + o) % 16
        return remote(r["gout"].at[to], r["gin"].at[k, z], r["a_s"].at[o], r["a_r"].at[o], plane(to))

    def a_from(o):
        src = (q + 16 - o) % 16
        return remote(r["gout"].at[q], r["gin"].at[src % 2, src // 2], r["a_s"].at[o], r["a_r"].at[o], plane(src))

    def n_copy(s, o):
        return remote(r["n_out"].at[s], r["n_in"].at[s, o], r["n_s"].at[s, o], r["n_r"].at[s, o], (rep, (me + o) % NS))

    def norm_start(s, g):
        total = jnp.sum(jnp.sum(g * g, axis=0, keepdims=True), axis=1, keepdims=True)
        r["n_out"][s] = jnp.broadcast_to(total, (1, 128))

        @pl.loop(1, NS)
        def _(o):
            n_copy(s, o).start()

    def clip_factor(s):
        @pl.loop(1, NS)
        def _(o):
            n_copy(s, o).wait_recv()

        acc = r["n_out"][s]
        for o in range(1, NS):
            acc = acc + r["n_in"][s, o]
        f = jnp.minimum(1.0, clip_norm / (jnp.sqrt(acc) + 1e-06))
        return f[:, :1].reshape(1, 1, 1)

    def ndot(a, b):
        return lax.dot_general(a, b, (((1,), (1,)), ((), ())), preferred_element_type=F32)

    g0_swap(1 - k).wait_recv()
    gt = ndot(r["gcol"][...].reshape(64, 512), r["wall"][...].reshape(256, 512))
    gt = (gt * scale - cross) * grad_scale
    norm_start(0, gt)
    r["gout"][...] = gt.T.astype(BF16).reshape(16, 16, 64)
    r["gin"][k, z] = r["gout"][q]

    @pl.loop(1, 16)
    def _(o):
        a_copy(o).start()

    ring_b.finish(r["tb"])
    peers = ((0, 1 - k), (1, k), (1, 1 - k))

    def c_copy(i):
        dy, kk = peers[i]
        yy = y if dy == 0 else 1 - y
        return remote(r["c_out"].at[i], r["c_in"].at[i], r["c_s"].at[i], r["c_r"].at[i], at(z, yy, kk))

    for i in (2, 1, 0):
        dy, kk = peers[i]
        yy = y if dy == 0 else 1 - y
        r["c_out"][i] = r["tb"][pl.ds(yy * 32 + kk * 16, 16), :].astype(BF16)
        c_copy(i).start()

    for o in (1, 7, 2, 6, 3, 5, 4):
        ag_copy(o, (z + NZ - o) % NZ).wait_recv()
        fw_copy(o, k).start()

    def adam(s, w, m, v, clipped):
        count = jnp.full((1, 8, 128), count_ref[0].astype(F32) + s, F32)
        one = (1.0 - jnp.exp(count * math.log(beta_one)))[:, :1, :1]
        two = (1.0 - jnp.exp(count * math.log(beta_two)))[:, :1, :1]
        m = beta_one * m + (1.0 - beta_one) * clipped
        v = beta_two * v + (1.0 - beta_two) * clipped * clipped
        update = m / one / (jnp.sqrt(v / two) + adam_eps)
        return w - inner_rate * (update + decay_rate * w), m, v

    def outer_step(theta, speed, weight_sum):
        delta = theta - weight_sum * (1.0 / n_rep)
        speed = outer_momentum * speed + delta
        return theta - outer_rate * (outer_momentum * speed + delta)

    theta0 = outer_step(
        jnp.where(lead, outer_ref[0], outer_ref[1]), jnp.where(lead, vel_ref[0], vel_ref[1]), rep_end(0)
    )

    @pl.loop(1, 16)
    def _(o):
        a_from(o).wait_recv()

    for zz in range(NZ):
        for f in range(2):
            r["g0"][f, :, 64 * zz : 64 * zz + 64] = r["gin"][f, zz].astype(F32)
    clipped = r["g0"][...] * clip_factor(0)
    w, m, v = adam(0, w, m, v, clipped)
    rep_start(1, jnp.where(lead, w[1], w[0]))
    a = jnp.where(lead, mixing * theta0 + (1.0 - mixing) * w[0], w[0])
    b = jnp.where(lead, w[1], mixing * theta0 + (1.0 - mixing) * w[1])
    w = jnp.stack([a, b])
    for o in range(NZ):
        fw_copy(o, 1 - k).wait_recv()
    prod = jnp.dot(w.reshape(32, 512).astype(BF16), r["gram"][...].reshape(512, 512), preferred_element_type=F32)
    for i in range(3):
        c_copy(i).wait_recv()
    r["c1"][k] = r["tb"][pl.ds(y * 32 + k * 16, 16), :] + r["c_in"][1].astype(F32)
    r["c1"][1 - k] = r["c_in"][0].astype(F32) + r["c_in"][2].astype(F32)
    g = (prod * scale - r["c1"][...].reshape(32, 512)) * grad_scale
    norm_start(1, g)
    rep_middle(1)
    clipped = g.reshape(2, 16, 512) * clip_factor(1)
    w, m, v = adam(1, w, m, v, clipped)
    theta1 = outer_step(
        jnp.where(lead, outer_ref[1], outer_ref[0]), jnp.where(lead, vel_ref[1], vel_ref[0]), rep_end(1)
    )
    out_ref[0] = jnp.where(lead, theta0, theta1)
    out_ref[1] = jnp.where(lead, theta1, theta0)
    out_ref[2] = jnp.where(lead, w[0], mixing * theta1 + (1.0 - mixing) * w[0])
    out_ref[3] = jnp.where(lead, mixing * theta1 + (1.0 - mixing) * w[1], w[1])

    core_a().wait_send()
    core_b().wait_send()
    ring_a.drain()
    ring_b.drain()
    w_swap().wait_send()
    for t in range(4):
        for d in range(2 if t < 3 else 1):
            w_copy(d, t, (z + NZ - t) % NZ if d == 0 else (z + t) % NZ).wait_send()
    for i in range(3):
        y_copy(i).wait_send()
        c_copy(i).wait_send()
    g0_swap(k).wait_send()
    for o in range(1, NZ):
        ag_copy(o, z).wait_send()
    for o in range(NZ):
        fw_copy(o, k).wait_send()

    @pl.loop(1, 16)
    def _(o):
        a_copy(o).wait_send()

    for s in range(2):

        @pl.loop(1, NS)
        def _(o):
            n_copy(s, o).wait_send()

        @pl.loop(1, n_rep)
        def _(o):
            rep_send_copy(s, o).wait_send()
            rep_back_copy(s, o, rep).wait_send()


SUB_A, SUB_B = 32, 32


def scratch_of(n_rep):
    vmem, dma = pltpu.VMEM, pltpu.SemaphoreType.DMA
    D = 512
    return (
        ("x", vmem((2, 512, D), BF16)),
        ("t", vmem((2, 512, 2, D), BF16)),
        ("pa", vmem((NK, NZ, 128, D), BF16)),
        ("pb", vmem((NK, NZ, 64, D), BF16)),
        ("ca", vmem((NZ, 128, D), BF16)),
        ("cb", vmem((NZ, 64, D), BF16)),
        ("ra_out", vmem((2, 7, 64, D), BF16)),
        ("ra_in", vmem((2, 7, 64, D), BF16)),
        ("rb_out", vmem((2, 7, 32, D), BF16)),
        ("rb_in", vmem((2, 7, 32, D), BF16)),
        ("ta", vmem((128, D), F32)),
        ("tb", vmem((64, D), F32)),
        ("wb", vmem((2, 16, D), BF16)),
        ("wall", vmem((NZ, NK, 16, D), BF16)),
        ("yc_out", vmem((64, 256), BF16)),
        ("yc_in", vmem((64, 256), BF16)),
        ("yg0_out", vmem((32, D), BF16)),
        ("yg0_in", vmem((32, D), BF16)),
        ("yg1_out", vmem((32, D), BF16)),
        ("yg1_in", vmem((32, D), BF16)),
        ("gcol", vmem((NK, 32, D), BF16)),
        ("gram", vmem((NZ, NK, 32, D), BF16)),
        ("gout", vmem((16, 16, 64), BF16)),
        ("gin", vmem((2, NZ, 16, 64), BF16)),
        ("g0", vmem((2, 16, D), F32)),
        ("c_out", vmem((3, 16, D), BF16)),
        ("c_in", vmem((3, 16, D), BF16)),
        ("c1", vmem((2, 16, D), F32)),
        ("n_out", vmem((2, 1, 128), F32)),
        ("n_in", vmem((2, NS, 1, 128), F32)),
        ("rep_out", vmem((2, n_rep, 1, D), F32)),
        ("rep_in", vmem((2, n_rep, 1, D), F32)),
        ("rep_all", vmem((2, n_rep, 1, D), F32)),
        ("state", vmem((5, 2, 16, D), F32)),
        ("load_state", dma((5,))),
        ("load", dma((2, 2))),
        ("core_s", dma((2,))),
        ("core_r", dma((2,))),
        ("ring_a_s", dma((2, 7, 64 // SUB_A))),
        ("ring_a_r", dma((2, 7, 64 // SUB_A))),
        ("ring_b_s", dma((2, 7, 32 // SUB_B))),
        ("ring_b_r", dma((2, 7, 32 // SUB_B))),
        ("wsw_s", dma),
        ("wsw_r", dma),
        ("w_s", dma((2, 4))),
        ("w_r", dma((2, 4))),
        ("y_s", dma((3,))),
        ("y_r", dma((3,))),
        ("gsw_s", dma),
        ("gsw_r", dma),
        ("ag_s", dma((NZ,))),
        ("ag_r", dma((NZ,))),
        ("fw_s", dma((NZ,))),
        ("fw_r", dma((NZ,))),
        ("a_s", dma((16,))),
        ("a_r", dma((16,))),
        ("c_s", dma((3,))),
        ("c_r", dma((3,))),
        ("n_s", dma((2, NS))),
        ("n_r", dma((2, NS))),
        ("rs_s", dma((2, n_rep))),
        ("rs_r", dma((2, n_rep))),
        ("ra_s", dma((2, n_rep))),
        ("ra_r", dma((2, n_rep))),
    )


def body(
    inner_weights,
    first_moment,
    second_moment,
    outer_weights,
    outer_velocity,
    tokens,
    targets,
    step_count,
    first_fragment,
):
    n_rep = lax.axis_size("rep")
    tok_dev, width = tokens.shape[2:]
    scale = 1.0 / math.sqrt(width)
    grad_scale = scale / (tok_dev * NS)
    vmem = pl.BlockSpec(memory_space=pltpu.VMEM)
    smem = pl.BlockSpec(memory_space=pltpu.SMEM)
    anywhere = pl.BlockSpec(memory_space=pl.ANY)
    out = pl.pallas_call(
        functools.partial(kernel, n_rep, scale, grad_scale),
        name="window",
        out_shape=jax.ShapeDtypeStruct((4, 16, width), F32),
        in_specs=[smem, smem] + [anywhere] * 7,
        out_specs=vmem,
        scratch_shapes=[shape for _, shape in scratch_of(n_rep)],
        compiler_params=pltpu.CompilerParams(collective_id=0, has_side_effects=True),
    )(
        step_count,
        first_fragment,
        tokens[0],
        targets[0],
        inner_weights[0],
        first_moment[0],
        second_moment[0],
        outer_weights,
        outer_velocity,
    )
    return out[:2], out[2:][None]


def solution(mesh):
    in_specs = (
        P("rep", None, "shard", None),
        P("rep", None, "shard", None),
        P("rep", None, "shard", None),
        P(None, "shard", None),
        P(None, "shard", None),
        P("rep", None, "shard", None),
        P("rep", None, "shard", None, None),
        P(),
        P(),
    )
    out_specs = (P(None, "shard", None), P("rep", None, "shard", None))
    return jax.shard_map(body, mesh=mesh, in_specs=in_specs, out_specs=out_specs, check_vma=False)
```

```python
import functools
import math

import jax
import jax.numpy as jnp
from jax import lax
from jax.experimental import pallas as pl
from jax.experimental.pallas import tpu as pltpu
from jax.sharding import PartitionSpec as P

beta_one = 0.9
beta_two = 0.95
inner_rate = 0.1
adam_eps = 1e-08
decay_rate = 0.1
clip_norm = 0.02
outer_rate = 0.7
outer_momentum = 0.9
mixing = 0.5

NZ, NY, NK = 8, 2, 2
NS = NZ * NY * NK
MESH = pl.DeviceIdType.MESH
F32, BF16 = jnp.float32, jnp.bfloat16


class Ring:
    def __init__(self, dev, mine, other, out, got, ss, rs, half, sub):
        self.dev, self.mine, self.other = dev, mine, other
        self.out, self.got, self.ss, self.rs = out, got, ss, rs
        self.half, self.sub = half, sub

    def copy(self, d, i, u):
        z, y, k, at, remote = self.dev
        zz = (z + 1) % NZ if d == 0 else (z + NZ - 1) % NZ
        rows = pl.ds(u * self.sub, self.sub)
        return remote(
            self.out.at[d, i, rows], self.got.at[d, i, rows], self.ss.at[d, i, u], self.rs.at[d, i, u], at(zz, y, k)
        )

    def own(self, owner, h, u):
        k = self.dev[2]
        rows = pl.ds(self.half * h + u * self.sub, self.sub)
        return self.mine[k, owner, rows, :].astype(F32) + self.other[owner, rows, :].astype(F32)

    def arrived(self, d, i, u):
        self.copy(d, i, u).wait_recv()
        return self.got[d, i, pl.ds(u * self.sub, self.sub), :].astype(F32)

    def step(self, t):
        z = self.dev[0]
        for long in (True, False):
            if not long and t == 3:
                continue
            hops = 4 if long else 3
            i = t if long else 4 + t
            for u in range(self.half // self.sub):
                for d in range(2):
                    h = d if long else 1 - d
                    owner = (z + hops - t) % NZ if d == 0 else (z + NZ - hops + t) % NZ
                    val = self.own(owner, h, u)
                    if t > 0:
                        val = val + self.arrived(d, i - 1, u)
                    self.out[d, i, pl.ds(u * self.sub, self.sub), :] = val.astype(BF16)
                    self.copy(d, i, u).start()

    def finish(self, total):
        z = self.dev[0]
        for u in range(self.half // self.sub):
            for h in range(2):
                val = self.own(z, h, u) + self.arrived(1 - h, 6, u) + self.arrived(h, 3, u)
                total[pl.ds(self.half * h + u * self.sub, self.sub), :] = val

    def drain(self):
        for d in range(2):
            for i in range(7):
                for u in range(self.half // self.sub):
                    self.copy(d, i, u).wait_send()


def kernel(n_rep, scale, grad_scale, count_ref, first_ref, x_hbm, t_hbm, w_hbm, m_hbm, v_hbm, outer_hbm, vel_hbm, out_ref, *scratch):
    names, shapes = zip(*scratch_of(n_rep))
    r = dict(zip(names, scratch, strict=True))
    state = (w_hbm, m_hbm, v_hbm, outer_hbm, vel_hbm)
    w_ref, m_ref, v_ref, outer_ref, vel_ref = (r["state"].at[i] for i in range(5))
    rep = lax.axis_index("rep")
    me = lax.axis_index("shard")
    z = me // 4
    y = (me // 2) % 2
    k = me % 2
    q = z * 2 + k

    def at(zz, yy, kk):
        return (rep, zz * 4 + yy * 2 + kk)

    def plane(qq):
        return at(qq // 2, y, qq % 2)

    partner = at(z, y, 1 - k)
    across = at(z, 1 - y, k)

    def remote(src, dst, ss, rs, dev):
        return pltpu.make_async_remote_copy(
            src_ref=src, dst_ref=dst, send_sem=ss, recv_sem=rs, device_id=dev, device_id_type=MESH
        )

    def load(s):
        return (
            pltpu.make_async_copy(x_hbm.at[s], r["x"].at[s], r["load"].at[s, 0]),
            pltpu.make_async_copy(t_hbm.at[s], r["t"].at[s], r["load"].at[s, 1]),
        )

    def load_state(i):
        return pltpu.make_async_copy(state[i], r["state"].at[i], r["load_state"].at[i])

    for c in load(0):
        c.start()
    for i in range(5):
        load_state(i).start()

    barrier = pltpu.get_barrier_semaphore()

    for dev in (partner, at((z + 1) % NZ, y, k), at((z + NZ - 1) % NZ, y, k), across):
        pl.semaphore_signal(barrier, inc=1, device_id=dev, device_id_type=MESH)

    @pl.loop(1, n_rep)
    def _(o):
        pl.semaphore_signal(barrier, inc=1, device_id=((rep + o) % n_rep, me), device_id_type=MESH)

    rep_out, rep_in, rep_all = r["rep_out"], r["rep_in"], r["rep_all"]

    def rep_send_copy(s, o):
        to = (rep + o) % n_rep
        return remote(rep_out.at[s, to], rep_in.at[s, o], r["rs_s"].at[s, o], r["rs_r"].at[s, o], (to, me))

    def rep_back_copy(s, o, row):
        to = (rep + o) % n_rep
        return remote(rep_all.at[s, row], rep_all.at[s, row], r["ra_s"].at[s, o], r["ra_r"].at[s, o], (to, me))

    def rep_start(s, value):
        rep_out[s] = value.reshape(n_rep, 1, value.shape[-1])

        @pl.loop(1, n_rep)
        def _(o):
            rep_send_copy(s, o).start()

    def rep_middle(s):
        @pl.loop(1, n_rep)
        def _(o):
            rep_send_copy(s, o).wait_recv()

        acc = rep_out[s, rep]
        for o in range(1, n_rep):
            acc = acc + rep_in[s, o]
        rep_all[s, rep] = acc

        @pl.loop(1, n_rep)
        def _(o):
            rep_back_copy(s, o, rep).start()

    def rep_end(s):
        @pl.loop(1, n_rep)
        def _(o):
            rep_back_copy(s, o, (rep + n_rep - o) % n_rep).wait_recv()

        return rep_all[s].reshape(n_rep, rep_all.shape[-1])

    def core_a():
        return remote(r["pa"].at[1 - k], r["ca"], r["core_s"].at[0], r["core_r"].at[0], partner)

    def core_b():
        return remote(r["pb"].at[1 - k], r["cb"], r["core_s"].at[1], r["core_r"].at[1], partner)

    dev = (z, y, k, at, remote)
    ring_a = Ring(dev, r["pa"], r["ca"], r["ra_out"], r["ra_in"], r["ring_a_s"], r["ring_a_r"], 64, SUB_A)
    ring_b = Ring(dev, r["pb"], r["cb"], r["rb_out"], r["rb_in"], r["ring_b_s"], r["ring_b_r"], 32, SUB_B)

    def tdot(a, b):
        return lax.dot_general(a, b, (((0,), (0,)), ((), ())), preferred_element_type=F32)

    def gram_rows(s, first_row):
        x = r["x"][s]
        xt = x.T
        g = jnp.dot(xt, x, preferred_element_type=F32).astype(BF16).reshape(NZ, NK, 32, 512)
        for kk in range(NK):
            r["pa"][kk, :, pl.ds(first_row, 32), :] = g[:, kk]
        return xt

    load(0)[0].wait()
    xt = gram_rows(0, 64)
    load(0)[1].wait()
    for c in load(1):
        c.start()
    flat = r["t"][0].reshape(512, 1024)
    for kk in range(NK):
        ct = jnp.dot(xt, flat[:, 512 * kk : 512 * kk + 512], preferred_element_type=F32)
        r["pa"][kk, :, pl.ds(0, 64), :] = ct.astype(BF16).reshape(NZ, 64, 512)
    for i in range(5):
        load_state(i).wait()
    w, m, v = w_ref[...], m_ref[...], v_ref[...]
    r["wb"][...] = w.astype(BF16)
    r["wall"][z, k] = r["wb"][k]
    for c in load(1):
        c.wait()
    gram_rows(1, 96)

    pl.semaphore_wait(barrier, 4 + n_rep - 1)
    core_a().start()

    def w_swap():
        return remote(r["wb"].at[1 - k], r["wall"].at[z, k], r["wsw_s"], r["wsw_r"], partner)

    def w_copy(d, t, block):
        zz = (z + 1) % NZ if d == 0 else (z + NZ - 1) % NZ
        return remote(r["wall"].at[block], r["wall"].at[block], r["w_s"].at[d, t], r["w_r"].at[d, t], at(zz, y, k))

    def w_step(t):
        if t == 0:
            remote(r["wb"].at[k], r["wall"].at[z, 1 - k], r["wsw_s"], r["wsw_r"], partner).wait_recv()
        for d in range(2 if t < 3 else 1):
            block = (z + NZ - t) % NZ if d == 0 else (z + t) % NZ
            if t > 0:
                w_copy(d, t - 1, block).wait_recv()
            w_copy(d, t, block).start()

    w_swap().start()
    lead = first_ref[0] == 0

    w_step(0)
    core_a().wait_recv()
    ring_a.step(0)
    w_step(1)
    flat = r["t"][1].reshape(512, 1024)
    for kk in range(NK):
        r["pb"][kk] = tdot(flat[:, 512 * kk : 512 * kk + 512], r["x"][1]).astype(BF16).reshape(NZ, 64, 512)
    core_b().start()
    ring_a.step(1)
    w_step(2)
    rep_start(0, jnp.where(lead, w[0], w[1]))
    ring_a.step(2)
    w_step(3)
    row = lax.broadcasted_iota(jnp.int32, (512, 256), 0)
    col = lax.broadcasted_iota(jnp.int32, (512, 256), 1)
    place = jnp.where((row // 64 == col // 32) & (row % 32 == col % 32), (row // 32) % 2, 2)
    pick_mine = jnp.where(place == y, 1.0, 0.0).astype(BF16)
    pick_other = jnp.where(place == 1 - y, 1.0, 0.0).astype(BF16)

    ring_a.step(3)
    core_b().wait_recv()
    ring_b.step(0)

    def y_copy(i):
        name = ("yc", "yg0", "yg1")[i]
        return remote(r[name + "_out"], r[name + "_in"], r["y_s"].at[i], r["y_r"].at[i], across)

    ring_a.finish(r["ta"])
    hi = r["ta"][pl.ds(0, 64), :].astype(BF16)
    lo = (r["ta"][pl.ds(0, 64), :] - hi.astype(F32)).astype(BF16)
    r["yc_out"][...] = jnp.dot(hi, pick_other, preferred_element_type=F32).astype(BF16)
    y_copy(0).start()
    r["yg0_out"][...] = r["ta"][pl.ds(64, 32), :].astype(BF16)
    y_copy(1).start()
    r["yg1_out"][...] = r["ta"][pl.ds(96, 32), :].astype(BF16)
    y_copy(2).start()
    ring_b.step(1)
    rep_middle(0)
    cross = jnp.dot(hi, pick_mine, preferred_element_type=F32) + jnp.dot(lo, pick_mine, preferred_element_type=F32)
    w_copy(0, 3, (z + NZ - 4) % NZ).wait_recv()
    w_copy(1, 2, (z + 3) % NZ).wait_recv()

    ring_b.step(2)

    def g0_swap(kk):
        return remote(r["gcol"].at[kk], r["gcol"].at[kk], r["gsw_s"], r["gsw_r"], partner)

    y_copy(0).wait_recv()
    cross = cross + r["yc_in"][...].astype(F32)
    y_copy(1).wait_recv()
    r["gcol"][k] = (r["ta"][pl.ds(64, 32), :] + r["yg0_in"][...].astype(F32)).astype(BF16)
    g0_swap(k).start()
    ring_b.step(3)

    def ag_copy(o, src):
        return remote(
            r["gram"].at[src, k], r["gram"].at[src, k], r["ag_s"].at[o], r["ag_r"].at[o], at((z + o) % NZ, y, k)
        )

    def fw_copy(o, kk):
        src = (z + NZ - o) % NZ
        return remote(r["gram"].at[src, kk], r["gram"].at[src, kk], r["fw_s"].at[o], r["fw_r"].at[o], partner)

    y_copy(2).wait_recv()
    r["gram"][z, k] = (r["ta"][pl.ds(96, 32), :] + r["yg1_in"][...].astype(F32)).astype(BF16)


    for o in (4, 3, 5, 2, 6, 1, 7):
        ag_copy(o, z).start()
    fw_copy(0, k).start()

    def a_copy(o):
        to = (q + o) % 16
        return remote(r["gout"].at[to], r["gin"].at[k, z], r["a_s"].at[o], r["a_r"].at[o], plane(to))

    def a_from(o):
        src = (q + 16 - o) % 16
        return remote(r["gout"].at[q], r["gin"].at[src % 2, src // 2], r["a_s"].at[o], r["a_r"].at[o], plane(src))

    def n_copy(s, o):
        return remote(r["n_out"].at[s], r["n_in"].at[s, o], r["n_s"].at[s, o], r["n_r"].at[s, o], (rep, (me + o) % NS))

    def norm_start(s, g):
        total = jnp.sum(jnp.sum(g * g, axis=0, keepdims=True), axis=1, keepdims=True)
        r["n_out"][s] = jnp.broadcast_to(total, (1, 128))

        @pl.loop(1, NS)
        def _(o):
            n_copy(s, o).start()

    def clip_factor(s):
        @pl.loop(1, NS)
        def _(o):
            n_copy(s, o).wait_recv()

        acc = r["n_out"][s]
        for o in range(1, NS):
            acc = acc + r["n_in"][s, o]
        f = jnp.minimum(1.0, clip_norm / (jnp.sqrt(acc) + 1e-06))
        return f[:, :1].reshape(1, 1, 1)

    def ndot(a, b):
        return lax.dot_general(a, b, (((1,), (1,)), ((), ())), preferred_element_type=F32)

    g0_swap(1 - k).wait_recv()
    gt = ndot(r["gcol"][...].reshape(64, 512), r["wall"][...].reshape(256, 512))
    gt = (gt * scale - cross) * grad_scale
    norm_start(0, gt)
    r["gout"][...] = gt.T.astype(BF16).reshape(16, 16, 64)
    r["gin"][k, z] = r["gout"][q]

    @pl.loop(1, 16)
    def _(o):
        a_copy(o).start()

    ring_b.finish(r["tb"])
    peers = ((0, 1 - k), (1, k), (1, 1 - k))

    def c_copy(i):
        dy, kk = peers[i]
        yy = y if dy == 0 else 1 - y
        return remote(r["c_out"].at[i], r["c_in"].at[i], r["c_s"].at[i], r["c_r"].at[i], at(z, yy, kk))

    for i in (2, 1, 0):
        dy, kk = peers[i]
        yy = y if dy == 0 else 1 - y
        r["c_out"][i] = r["tb"][pl.ds(yy * 32 + kk * 16, 16), :].astype(BF16)
        c_copy(i).start()

    for o in (1, 7, 2, 6, 3, 5, 4):
        ag_copy(o, (z + NZ - o) % NZ).wait_recv()
        fw_copy(o, k).start()

    def adam(s, w, m, v, clipped):
        count = jnp.full((1, 8, 128), count_ref[0].astype(F32) + s, F32)
        one = (1.0 - jnp.exp(count * math.log(beta_one)))[:, :1, :1]
        two = (1.0 - jnp.exp(count * math.log(beta_two)))[:, :1, :1]
        m = beta_one * m + (1.0 - beta_one) * clipped
        v = beta_two * v + (1.0 - beta_two) * clipped * clipped
        update = m / one / (jnp.sqrt(v / two) + adam_eps)
        return w - inner_rate * (update + decay_rate * w), m, v

    def outer_step(theta, speed, weight_sum):
        delta = theta - weight_sum * (1.0 / n_rep)
        speed = outer_momentum * speed + delta
        return theta - outer_rate * (outer_momentum * speed + delta)

    theta0 = outer_step(
        jnp.where(lead, outer_ref[0], outer_ref[1]), jnp.where(lead, vel_ref[0], vel_ref[1]), rep_end(0)
    )

    @pl.loop(1, 16)
    def _(o):
        a_from(o).wait_recv()

    for zz in range(NZ):
        for f in range(2):
            r["g0"][f, :, 64 * zz : 64 * zz + 64] = r["gin"][f, zz].astype(F32)
    clipped = r["g0"][...] * clip_factor(0)
    w, m, v = adam(0, w, m, v, clipped)
    rep_start(1, jnp.where(lead, w[1], w[0]))
    a = jnp.where(lead, mixing * theta0 + (1.0 - mixing) * w[0], w[0])
    b = jnp.where(lead, w[1], mixing * theta0 + (1.0 - mixing) * w[1])
    w = jnp.stack([a, b])
    for o in range(NZ):
        fw_copy(o, 1 - k).wait_recv()
    prod = jnp.dot(w.reshape(32, 512).astype(BF16), r["gram"][...].reshape(512, 512), preferred_element_type=F32)
    for i in range(3):
        c_copy(i).wait_recv()
    r["c1"][k] = r["tb"][pl.ds(y * 32 + k * 16, 16), :] + r["c_in"][1].astype(F32)
    r["c1"][1 - k] = r["c_in"][0].astype(F32) + r["c_in"][2].astype(F32)
    g = (prod * scale - r["c1"][...].reshape(32, 512)) * grad_scale
    norm_start(1, g)
    rep_middle(1)
    core_a().wait_send()
    core_b().wait_send()
    ring_a.drain()
    ring_b.drain()
    w_swap().wait_send()
    for t in range(4):
        for d in range(2 if t < 3 else 1):
            w_copy(d, t, (z + NZ - t) % NZ if d == 0 else (z + t) % NZ).wait_send()
    for i in range(3):
        y_copy(i).wait_send()
        c_copy(i).wait_send()
    g0_swap(k).wait_send()
    for o in range(1, NZ):
        ag_copy(o, z).wait_send()
    for o in range(NZ):
        fw_copy(o, k).wait_send()

    @pl.loop(1, 16)
    def _(o):
        a_copy(o).wait_send()

    def drain_sums(s):
        @pl.loop(1, NS)
        def _(o):
            n_copy(s, o).wait_send()

        @pl.loop(1, n_rep)
        def _(o):
            rep_send_copy(s, o).wait_send()
            rep_back_copy(s, o, rep).wait_send()

    drain_sums(0)
    clipped = g.reshape(2, 16, 512) * clip_factor(1)
    w, m, v = adam(1, w, m, v, clipped)
    theta1 = outer_step(
        jnp.where(lead, outer_ref[1], outer_ref[0]), jnp.where(lead, vel_ref[1], vel_ref[0]), rep_end(1)
    )
    out_ref[0] = jnp.where(lead, theta0, theta1)
    out_ref[1] = jnp.where(lead, theta1, theta0)
    out_ref[2] = jnp.where(lead, w[0], mixing * theta1 + (1.0 - mixing) * w[0])
    out_ref[3] = jnp.where(lead, mixing * theta1 + (1.0 - mixing) * w[1], w[1])

    drain_sums(1)


SUB_A, SUB_B = 64, 32


def scratch_of(n_rep):
    vmem, dma = pltpu.VMEM, pltpu.SemaphoreType.DMA
    D = 512
    return (
        ("x", vmem((2, 512, D), BF16)),
        ("t", vmem((2, 512, 2, D), BF16)),
        ("pa", vmem((NK, NZ, 128, D), BF16)),
        ("pb", vmem((NK, NZ, 64, D), BF16)),
        ("ca", vmem((NZ, 128, D), BF16)),
        ("cb", vmem((NZ, 64, D), BF16)),
        ("ra_out", vmem((2, 7, 64, D), BF16)),
        ("ra_in", vmem((2, 7, 64, D), BF16)),
        ("rb_out", vmem((2, 7, 32, D), BF16)),
        ("rb_in", vmem((2, 7, 32, D), BF16)),
        ("ta", vmem((128, D), F32)),
        ("tb", vmem((64, D), F32)),
        ("wb", vmem((2, 16, D), BF16)),
        ("wall", vmem((NZ, NK, 16, D), BF16)),
        ("yc_out", vmem((64, 256), BF16)),
        ("yc_in", vmem((64, 256), BF16)),
        ("yg0_out", vmem((32, D), BF16)),
        ("yg0_in", vmem((32, D), BF16)),
        ("yg1_out", vmem((32, D), BF16)),
        ("yg1_in", vmem((32, D), BF16)),
        ("gcol", vmem((NK, 32, D), BF16)),
        ("gram", vmem((NZ, NK, 32, D), BF16)),
        ("gout", vmem((16, 16, 64), BF16)),
        ("gin", vmem((2, NZ, 16, 64), BF16)),
        ("g0", vmem((2, 16, D), F32)),
        ("c_out", vmem((3, 16, D), BF16)),
        ("c_in", vmem((3, 16, D), BF16)),
        ("c1", vmem((2, 16, D), F32)),
        ("n_out", vmem((2, 1, 128), F32)),
        ("n_in", vmem((2, NS, 1, 128), F32)),
        ("rep_out", vmem((2, n_rep, 1, D), F32)),
        ("rep_in", vmem((2, n_rep, 1, D), F32)),
        ("rep_all", vmem((2, n_rep, 1, D), F32)),
        ("state", vmem((5, 2, 16, D), F32)),
        ("load_state", dma((5,))),
        ("load", dma((2, 2))),
        ("core_s", dma((2,))),
        ("core_r", dma((2,))),
        ("ring_a_s", dma((2, 7, 64 // SUB_A))),
        ("ring_a_r", dma((2, 7, 64 // SUB_A))),
        ("ring_b_s", dma((2, 7, 32 // SUB_B))),
        ("ring_b_r", dma((2, 7, 32 // SUB_B))),
        ("wsw_s", dma),
        ("wsw_r", dma),
        ("w_s", dma((2, 4))),
        ("w_r", dma((2, 4))),
        ("y_s", dma((3,))),
        ("y_r", dma((3,))),
        ("gsw_s", dma),
        ("gsw_r", dma),
        ("ag_s", dma((NZ,))),
        ("ag_r", dma((NZ,))),
        ("fw_s", dma((NZ,))),
        ("fw_r", dma((NZ,))),
        ("a_s", dma((16,))),
        ("a_r", dma((16,))),
        ("c_s", dma((3,))),
        ("c_r", dma((3,))),
        ("n_s", dma((2, NS))),
        ("n_r", dma((2, NS))),
        ("rs_s", dma((2, n_rep))),
        ("rs_r", dma((2, n_rep))),
        ("ra_s", dma((2, n_rep))),
        ("ra_r", dma((2, n_rep))),
    )


def body(
    inner_weights,
    first_moment,
    second_moment,
    outer_weights,
    outer_velocity,
    tokens,
    targets,
    step_count,
    first_fragment,
):
    n_rep = lax.axis_size("rep")
    tok_dev, width = tokens.shape[2:]
    scale = 1.0 / math.sqrt(width)
    grad_scale = scale / (tok_dev * NS)
    vmem = pl.BlockSpec(memory_space=pltpu.VMEM)
    smem = pl.BlockSpec(memory_space=pltpu.SMEM)
    anywhere = pl.BlockSpec(memory_space=pl.ANY)
    out = pl.pallas_call(
        functools.partial(kernel, n_rep, scale, grad_scale),
        name="window",
        out_shape=jax.ShapeDtypeStruct((4, 16, width), F32),
        in_specs=[smem, smem] + [anywhere] * 7,
        out_specs=vmem,
        scratch_shapes=[shape for _, shape in scratch_of(n_rep)],
        compiler_params=pltpu.CompilerParams(collective_id=0, has_side_effects=True),
    )(
        step_count,
        first_fragment,
        tokens[0],
        targets[0],
        inner_weights[0],
        first_moment[0],
        second_moment[0],
        outer_weights,
        outer_velocity,
    )
    return out[:2], out[2:][None]


def solution(mesh):
    in_specs = (
        P("rep", None, "shard", None),
        P("rep", None, "shard", None),
        P("rep", None, "shard", None),
        P(None, "shard", None),
        P(None, "shard", None),
        P("rep", None, "shard", None),
        P("rep", None, "shard", None, None),
        P(),
        P(),
    )
    out_specs = (P(None, "shard", None), P("rep", None, "shard", None))
    return jax.shard_map(body, mesh=mesh, in_specs=in_specs, out_specs=out_specs, check_vma=False)
```
